1024 devices in a mesh: gx: 16 (over z, core), gy: 16 (over y_lo, x), gz: 4 (over y_hi).
Axes of the slice: x: 8, y: 8 (y_hi: 4, y_lo: 2; y = y_hi * 2 + y_lo), z: 8, core: 2. Of those that a mesh axis runs over, the one named last changes fastest.
Arguments:
- links: bfloat16 [16, 16, 32, 2, 9, 64, 128], P('gx', 'gy', 'gz'), may hold values from -0.5 to 0.5
- null_vectors: bfloat16 [16, 16, 32, 2, 32, 128], P('gx', 'gy', 'gz'), may hold values from -1.796875 to 1.796875
- offsets: int32 [9, 4], replicated, may hold values from -1 to 1, as said below
- place: int32 [8, 8, 16, 1], replicated, may hold values from 0 to 31, as said below
Outputs:
- coarse_links: float32 [16, 4, 16, 9, 2048], P('gx', 'gz')
The draws below stay inside these ranges and needn't reach their ends.
Inputs may be any that keep to these rules, and one draw needn't show every extreme that they name: The rows are the nine offsets zero, plus one and minus one along each of x, y, z, t, each once, in some order. `place`: for each cx and each aligned run of 4 values of cz, the values over all cy, those cz and all ct are each of 0 to 31 once.
All inputs are finite; a program needn't handle non-finite values.
Results may differ from the reference program's by a relative error of at most 0.0029.
Values may be sent and summed in bfloat16 or wider, within the bound.
No kernel may reach another device: no remote copies, remote signals or barrier semaphores. Data moves between devices by JAX's collectives and lax.ppermute only.
A program may use at most 32 MiB of HBM per device.

```python
import jax
import jax.numpy as jnp
from jax import lax

NC = 64
NV = 32
ZL = 8
TL = 2
NX = 16
NY = 16
NZ = 32
CX = 8
CY = 8
CZ = 16
CT = 1
CAP = 16
N_GX = 16
N_GZ = 4


STENCIL = ((0, 0, 0, 0), (1, 0, 0, 0), (-1, 0, 0, 0), (0, 1, 0, 0), (0, -1, 0, 0), (0, 0, 1, 0), (0, 0, -1, 0), (0, 0, 0, 1), (0, 0, 0, -1))


def draw_offsets(key, part):
    standard_table = jnp.array(STENCIL, jnp.int32)
    return jax.random.permutation(jax.random.fold_in(key, 11), standard_table).astype(jnp.int32)


def draw_place(key, part):
    block_count = CZ // (ZL // 2)
    line_size = CY * (ZL // 2) * CT
    key_list = jax.random.split(jax.random.fold_in(key, 23), CX * block_count)
    permuted = jax.vmap(lambda single: jax.random.permutation(single, line_size))(key_list)
    permuted = permuted.reshape(CX, block_count, CY, ZL // 2, CT)
    permuted = jnp.transpose(permuted, (0, 2, 1, 3, 4)).reshape(CX, CY, CZ, CT)
    return permuted.astype(jnp.int32)


def steps_of(own_key, extent, pieces, least, high):
    gain, own = 1.0, jax.random.fold_in(own_key, 6)
    for position, parts in pieces:
        draws = jnp.exp(jax.random.uniform(jax.random.fold_in(own, position), (parts,), jnp.float32, least / len(pieces), high / len(pieces)))
        gain = gain * jnp.repeat(draws, extent[position] // parts).reshape([-1 if axis == position else 1 for axis in range(len(extent))])
    return gain


def bell_draw(key, extent, deviation, limit, cuts=(), held_as=jnp.bfloat16):
    drawn = deviation * jax.random.normal(key, extent, jnp.float32)
    if cuts:
        drawn = drawn * steps_of(key, extent, cuts, -0.22, 0.18)
    return jnp.clip(drawn, -limit, limit).astype(held_as)


def setup_inputs(seed: int = 0) -> dict:
    splits = jax.random.split(jax.random.key(seed), 5)
    return {
        "links": bell_draw(splits[0], (NX, NY, NZ, TL, 9, NC, 2 * NC), (2 * NC) ** -0.5, 0.5, ((0, 16), (1, 16), (2, 4))),
        "null_vectors": bell_draw(splits[1], (NX, NY, NZ, TL, NV, 2 * NC), 0.3, 1.796875, ((0, 16), (1, 16), (2, 4))),
        "offsets": draw_offsets(jax.random.fold_in(splits[4], 71), 0),
        "place": draw_place(jax.random.fold_in(splits[4], 71), 0),
    }


def neighbour_blocks(neighbour):
    half_width = neighbour.shape[-1] // 2
    real_part = neighbour[..., :half_width]
    imag_part = neighbour[..., half_width:]
    upper_rows = jnp.concatenate([real_part, -imag_part], -1)
    lower_rows = jnp.concatenate([imag_part, real_part], -1)
    return jnp.concatenate([upper_rows, lower_rows], -2)


def conj_blocks(hopped):
    half_width = hopped.shape[-1] // 2
    hop_real = hopped[..., :half_width]
    hop_imag = hopped[..., half_width:]
    return jnp.concatenate([hopped, jnp.concatenate([hop_imag, -hop_real], -1)], -2)


def reference(links, null_vectors, offsets, place):
    x_count = links.shape[0]
    y_count = links.shape[1]
    z_count = links.shape[2]
    t_count = links.shape[3]
    vec_count = null_vectors.shape[4]
    flat_width = 2 * vec_count * vec_count
    y_parity = (jnp.arange(y_count, dtype=jnp.int32) % 2) * 2 - 1
    z_parity = (jnp.arange(z_count, dtype=jnp.int32) % 2) * 2 - 1
    t_parity = (jnp.arange(t_count, dtype=jnp.int32) % 2) * 2 - 1
    is_self = jnp.all(offsets == 0, axis=1).astype(jnp.float32)

    def one_slice(x_index):
        link_slice = lax.dynamic_index_in_dim(links, x_index, 0, False).astype(jnp.float32)
        own_vectors = lax.dynamic_index_in_dim(null_vectors, x_index, 0, False).astype(jnp.float32)
        x_sign = (x_index % 2) * 2 - 1
        term_list = []
        outside_list = []
        for direction in range(9):
            offset_row = offsets[direction]
            source = ((x_index + offset_row[0]) % x_count).astype(jnp.int32)
            neighbour = lax.dynamic_index_in_dim(null_vectors, source, 0, False)
            neighbour = jnp.roll(neighbour, -offset_row[1], axis=0)
            neighbour = jnp.roll(neighbour, -offset_row[2], axis=1)
            neighbour = jnp.roll(neighbour, -offset_row[3], axis=2)
            hopped = jnp.einsum('yztrc,yztuc->yztru', link_slice[:, :, :, direction],
                                neighbour_blocks(neighbour).astype(jnp.float32))
            hopped = lax.optimization_barrier(hopped.astype(jnp.bfloat16)).astype(jnp.float32)
            term = jnp.einsum('yztvq,yztqu->yztvu', own_vectors, conj_blocks(hopped))
            outside = ((offset_row[0] == x_sign).astype(jnp.float32)
                       + (offset_row[1] == y_parity).astype(jnp.float32)[:, None, None]
                       + (offset_row[2] == z_parity).astype(jnp.float32)[None, :, None]
                       + (offset_row[3] == t_parity).astype(jnp.float32)[None, None, :])
            term_list.append(term)
            outside_list.append(outside)
        spilled = jnp.zeros_like(term_list[0])
        for direction in range(9):
            spilled = spilled + (1.0 - outside_list[direction])[..., None, None] * term_list[direction]
        contrib = []
        for direction in range(9):
            contrib.append(outside_list[direction][..., None, None] * term_list[direction]
                           + is_self[direction] * spilled)
        stacked = jnp.stack(contrib)
        stacked = stacked.reshape(9, y_count // 2, 2, z_count // 2, 2, t_count // 2, 2, vec_count, 2 * vec_count)
        return stacked.sum(axis=(2, 4, 6))

    per_x = lax.map(one_slice, jnp.arange(x_count, dtype=jnp.int32))
    coarse = per_x.reshape((x_count // 2, 2) + per_x.shape[1:]).sum(axis=1)
    coarse = jnp.transpose(coarse, (0, 2, 3, 4, 1, 5, 6)).reshape(CX, CY, CZ, CT, 9, flat_width)
    target_x = 2 * jnp.arange(CX, dtype=jnp.int32)[:, None, None, None] + place // CAP
    block_z = jnp.broadcast_to((jnp.arange(CZ, dtype=jnp.int32) // (ZL // 2))[None, None, :, None], place.shape)
    slot_index = place % CAP
    result = jnp.zeros((N_GX, N_GZ, CAP, 9, flat_width), jnp.float32)
    return result.at[target_x.astype(jnp.int32), block_z.astype(jnp.int32), slot_index.astype(jnp.int32)].set(coarse)
```

```python
import jax
import jax.numpy as jnp
from jax import lax
from jax.experimental import pallas as pl
from jax.experimental.pallas import tpu as pltpu
from jax.sharding import Mesh, PartitionSpec as P

F32 = jnp.float32
BF16 = jnp.bfloat16
GX = ("xh", "xl")
GY = ("yl", "yh", "yp")


def swap_inner(count):
    return [(i, i ^ 1) for i in range(count)]


def swap_outer(count):
    pairs = []
    for i in range(count):
        step = 1 if i % 2 else -1
        pairs.append((i, (i + step) % count))
    return pairs


def shift(count, step):
    return [(i, (i + step) % count) for i in range(count)]


def lane_low(shape):
    return lax.broadcasted_iota(jnp.int32, shape, 1) < 64


def block_of(vectors):
    wide = vectors.astype(F32)
    upper = jnp.where(lane_low(wide.shape), wide, -wide)
    lower = pltpu.roll(wide, 64, 1)
    return jnp.concatenate(
        [upper.astype(BF16), lower.astype(BF16), lower.astype(BF16), (-upper).astype(BF16)], 0
    )


def hop(link_block, rows):
    out = lax.dot_general(link_block, rows, (((1,), (1,)), ((), ())), preferred_element_type=F32)
    return out.astype(BF16)


def project(own, stacked):
    return jnp.dot(own, stacked, preferred_element_type=F32)


def fold(result):
    low = lane_low((16, 128))
    first = jnp.where(low, result[0:16], result[48:64])
    second = jnp.where(low, result[16:32], result[32:48])
    return first + pltpu.roll(second, 64, 1)


def hop_kernel(
    off_ref, links_ref, v_ref, xa_ref, xb_ref, ya_ref, yb_ref, zl_ref, zh_ref, out_ref, vf_ref, rows_ref
):
    def find(axis, sign):
        index = jnp.int32(0)
        for k in range(9):
            index = index + jnp.where(off_ref[k, axis] == sign, k, 0).astype(jnp.int32)
        return index

    k_self = jnp.int32(36)
    minus = [find(axis, -1) for axis in range(4)]
    plus = [find(axis, 1) for axis in range(4)]
    for axis in range(4):
        k_self = k_self - minus[axis] - plus[axis]
    x_odd = lax.axis_index("xl") == 1
    y_odd = lax.axis_index("yp") == 1
    x_out = jnp.where(x_odd, plus[0], minus[0])
    x_in = jnp.where(x_odd, minus[0], plus[0])
    y_out = jnp.where(y_odd, plus[1], minus[1])
    y_in = jnp.where(y_odd, minus[1], plus[1])

    for z in range(8):
        for t in range(2):
            vf_ref[pl.ds((2 * z + t) * 32, 32), :] = v_ref[z, t].astype(F32)
            rows_ref[2 * z + t] = block_of(v_ref[z, t])

    low = lane_low((16, 128))
    low_own = lane_low((64, 128))
    zero = jnp.zeros((16, 128), BF16)
    for agg in range(4):
        halves = []
        for zz in range(2):
            base = (2 * (2 * agg + zz)) * 32
            quarter = []
            for first in range(2):
                left = vf_ref[pl.ds(base + first, 16, stride=2), :]
                right = vf_ref[pl.ds(base + 32 + first, 16, stride=2), :]
                quarter.append(
                    (
                        jnp.where(low, left, pltpu.roll(right, 64, 1)),
                        jnp.where(low, pltpu.roll(left, 64, 1), right),
                    )
                )
            half = jnp.concatenate([quarter[0][0], quarter[1][0], quarter[0][1], quarter[1][1]], 0)
            halves.append(half)
        own = jnp.concatenate([h.astype(BF16) for h in halves], 1)
        own_t0 = jnp.concatenate([jnp.where(low_own, h, 0.0).astype(BF16) for h in halves], 1)
        own_t1 = jnp.concatenate([jnp.where(low_own, 0.0, h).astype(BF16) for h in halves], 1)

        sites = [(2 * agg + zz, t) for zz in range(2) for t in range(2)]
        g_self, g_tin, g_tout, g_zin, g_zout = {}, {}, {}, {}, {}
        for z, t in sites:
            k_tin = plus[3] if t == 1 else minus[3]
            k_tout = minus[3] if t == 1 else plus[3]
            k_zin = minus[2] if z % 2 == 0 else plus[2]
            stack = jnp.concatenate(
                [
                    links_ref[z, t, k_self],
                    links_ref[z, 1 - t, k_tin],
                    links_ref[z, 1 - t, k_tout],
                    links_ref[z ^ 1, t, k_zin],
                ],
                0,
            )
            res = hop(stack, rows_ref[2 * z + t])
            g_self[(z, t)] = res[0:64]
            g_tin[(z, 1 - t)] = res[64:128]
            g_tout[(z, 1 - t)] = res[128:192]
            g_zin[(z ^ 1, t)] = res[192:256]
        for z, t in sites:
            if z % 2 == 0:
                k_zout, target = minus[2], z - 1
            else:
                k_zout, target = plus[2], z + 1
            if target < 0:
                rows = block_of(zl_ref[0, t])
            elif target > 7:
                rows = block_of(zh_ref[0, t])
            else:
                rows = rows_ref[2 * target + t]
            g_zout[(z, t)] = hop(links_ref[z, t, k_zout], rows)

        def cat(table):
            return jnp.concatenate([table[s] for s in sites], 0)

        def halo(ref, k):
            return jnp.concatenate([hop(links_ref[z, t, k], block_of(ref[z, t])) for z, t in sites], 0)

        total = project(own, cat(g_self))
        total = total + project(own, cat(g_tin))
        total = total + project(own, cat(g_zin))
        total = total + project(own, halo(xa_ref, x_in))
        total = total + project(own, halo(ya_ref, y_in))
        out_ref[agg, k_self] = fold(total).astype(BF16)
        out_ref[agg, x_out] = fold(project(own, halo(xb_ref, x_out))).astype(BF16)
        out_ref[agg, y_out] = fold(project(own, halo(yb_ref, y_out))).astype(BF16)
        out_ref[agg, x_in] = zero
        out_ref[agg, y_in] = zero
        z_out = cat(g_zout)
        out_ref[agg, minus[2]] = fold(project(own[:, :128], z_out[:128])).astype(BF16)
        out_ref[agg, plus[2]] = fold(project(own[:, 128:], z_out[128:])).astype(BF16)
        t_out = cat(g_tout)
        out_ref[agg, minus[3]] = fold(project(own_t0, t_out)).astype(BF16)
        out_ref[agg, plus[3]] = fold(project(own_t1, t_out)).astype(BF16)


def place_kernel(place_ref, own_ref, other_ref, out_ref, table_ref, wide_ref):
    line = lax.axis_index("xh")
    column = lax.axis_index("xl")
    block = lax.axis_index("gz")

    def note(entry, carry):
        cy = entry // 4
        target = place_ref[line, cy, block * 4 + entry % 4]
        table_ref[target] = entry
        return carry

    lax.fori_loop(0, 32, note, 0, unroll=True)

    def emit(slot, carry):
        entry = table_ref[column * 16 + slot]
        source = 2 * (entry // 4) + entry % 2
        is_own = (entry % 4) // 2 == column
        wide_ref[...] = jnp.where(
            is_own, own_ref[source].astype(F32), other_ref[source].astype(F32)
        ).reshape(144, 128)
        for lane in range(16):
            out_ref[slot, :, lane * 128 : (lane + 1) * 128] = wide_ref[pl.ds(lane, 9, stride=16), :]
        return carry

    lax.fori_loop(0, 16, emit, 0)


def local(links, null_vectors, offsets, place):
    own = null_vectors[0, 0]
    links = links[0, 0]
    z_low = lax.ppermute(own[7:8], "gz", shift(4, 1))
    z_high = lax.ppermute(own[0:1], "gz", shift(4, -1))
    x_inner = lax.ppermute(own, "xl", swap_inner(2))
    x_outer = lax.ppermute(own, GX, swap_outer(16))
    y_inner = lax.ppermute(own, "yp", swap_inner(2))
    y_outer = lax.ppermute(own, GY, swap_outer(16))
    vmem = pl.BlockSpec(memory_space=pltpu.VMEM)
    smem = pl.BlockSpec(memory_space=pltpu.SMEM)
    partial_value = pl.pallas_call(
        hop_kernel,
        out_shape=jax.ShapeDtypeStruct((4, 9, 16, 128), BF16),
        in_specs=[smem] + [vmem] * 8,
        out_specs=vmem,
        scratch_shapes=[pltpu.VMEM((512, 128), F32), pltpu.VMEM((16, 128, 128), BF16)],
        compiler_params=pltpu.CompilerParams(vmem_limit_bytes=32 * 1024 * 1024),
        cost_estimate=pl.CostEstimate(flops=300_000_000, bytes_accessed=4_000_000, transcendentals=0),
        name="hop",
    )(offsets, links, own, x_inner, x_outer, y_inner, y_outer, z_low, z_high)
    parts = lax.all_to_all(partial_value, ("xl", "yp"), 0, 0, tiled=True)
    chunk = jnp.sum(parts.astype(F32), axis=0).astype(BF16)
    spread = jnp.broadcast_to(chunk[None], (16, 9, 16, 128))
    mine = lax.all_to_all(spread, GY, 0, 0, tiled=True)
    other = lax.ppermute(mine, "xl", swap_inner(2))
    placed = pl.pallas_call(
        place_kernel,
        out_shape=jax.ShapeDtypeStruct((16, 9, 2048), F32),
        in_specs=[smem, vmem, vmem],
        out_specs=vmem,
        scratch_shapes=[pltpu.SMEM((32,), jnp.int32), pltpu.VMEM((144, 128), F32)],
        compiler_params=pltpu.CompilerParams(vmem_limit_bytes=32 * 1024 * 1024),
        name="place",
    )(place.reshape(8, 8, 16), mine, other)
    return placed[None, None]


def solution(mesh):
    fine = Mesh(mesh.devices.reshape(8, 2, 2, 4, 2, 4), ("xh", "xl", "yl", "yh", "yp", "gz"))
    placed = (P(GX, GY, "gz"), P(GX, GY, "gz"), P(), P())
    return jax.shard_map(
        local,
        mesh=fine,
        in_specs=placed,
        out_specs=P(GX, "gz"),
        check_vma=False,
    )
```

```python
import jax
import jax.numpy as jnp
from jax import lax
from jax.experimental import pallas as pl
from jax.experimental.pallas import tpu as pltpu
from jax.sharding import Mesh, PartitionSpec as P

F32 = jnp.float32
BF16 = jnp.bfloat16
GX = ("xh", "xl")
GY = ("yl", "yh", "yp")


def swap_inner(count):
    return [(i, i ^ 1) for i in range(count)]


def swap_outer(count):
    pairs = []
    for i in range(count):
        step = 1 if i % 2 else -1
        pairs.append((i, (i + step) % count))
    return pairs


def shift(count, step):
    return [(i, (i + step) % count) for i in range(count)]


def lane_index(shape):
    return lax.broadcasted_iota(jnp.int32, shape, 1)


def block_of(vectors):
    wide = vectors.astype(F32)
    upper = jnp.where(lane_index(wide.shape) < 64, wide, -wide)
    lower = pltpu.roll(wide, 64, 1)
    return jnp.concatenate([upper.astype(BF16), lower.astype(BF16)], 0)


def hop(link_block, rows):
    out = lax.dot_general(link_block, rows, (((1,), (1,)), ((), ())), preferred_element_type=F32)
    return out.astype(BF16)


def project(own, stacked):
    return jnp.dot(own, stacked, preferred_element_type=F32)


def fold(result):
    first = jnp.concatenate([result[0:16], result[16:32]], 1)
    second = jnp.concatenate([result[32:48], result[48:64]], 1)
    low = lane_index((16, 128)) % 64 < 32
    return first + jnp.where(low, pltpu.roll(second, 96, 1), -pltpu.roll(second, 32, 1))


def roles_of(off_ref):
    def find(axis, sign):
        index = jnp.int32(0)
        for k in range(9):
            index = index + jnp.where(off_ref[axis, k] == sign, k, 0).astype(jnp.int32)
        return index

    minus = [find(axis, -1) for axis in range(4)]
    plus = [find(axis, 1) for axis in range(4)]
    k_self = jnp.int32(36)
    for axis in range(4):
        k_self = k_self - minus[axis] - plus[axis]
    return k_self, minus, plus


def sites_of(agg):
    return [(2 * agg + zz, t) for zz in range(2) for t in range(2)]


def inside_kernel(off_ref, links_ref, v_ref, part_ref, acc_ref, own_ref, vf_ref, rows_ref):
    k_self, minus, plus = roles_of(off_ref)
    for z in range(8):
        for t in range(2):
            vf_ref[pl.ds((2 * z + t) * 32, 32), :] = v_ref[z, t].astype(F32)
            rows_ref[2 * z + t] = block_of(v_ref[z, t])

    low = lane_index((16, 128)) < 64
    low_own = lane_index((64, 128)) < 64
    for agg in range(4):
        halves = []
        for zz in range(2):
            base = (2 * (2 * agg + zz)) * 32
            quarter = []
            for first in range(2):
                left = vf_ref[pl.ds(base + first, 16, stride=2), :]
                right = vf_ref[pl.ds(base + 32 + first, 16, stride=2), :]
                quarter.append(
                    (
                        jnp.where(low, left, pltpu.roll(right, 64, 1)),
                        jnp.where(low, pltpu.roll(left, 64, 1), right),
                    )
                )
            half = jnp.concatenate([quarter[0][0], quarter[1][0], quarter[0][1], quarter[1][1]], 0)
            halves.append(half)
        own = jnp.concatenate([h.astype(BF16) for h in halves], 1)
        own_ref[agg] = own
        own_t0 = jnp.concatenate([jnp.where(low_own, h, 0.0).astype(BF16) for h in halves], 1)
        own_t1 = jnp.concatenate([jnp.where(low_own, 0.0, h).astype(BF16) for h in halves], 1)

        sites = sites_of(agg)
        g_self, g_tin, g_tout, g_zin = {}, {}, {}, {}
        for z, t in sites:
            k_tin = plus[3] if t == 1 else minus[3]
            k_tout = minus[3] if t == 1 else plus[3]
            k_zin = minus[2] if z % 2 == 0 else plus[2]
            stack = jnp.concatenate(
                [
                    links_ref[z, t, k_self],
                    links_ref[z, 1 - t, k_tin],
                    links_ref[z, 1 - t, k_tout],
                    links_ref[z ^ 1, t, k_zin],
                ],
                0,
            )
            res = hop(stack, rows_ref[2 * z + t])
            g_self[(z, t)] = res[0:64]
            g_tin[(z, 1 - t)] = res[64:128]
            g_tout[(z, 1 - t)] = res[128:192]
            g_zin[(z ^ 1, t)] = res[192:256]

        def cat(table):
            return jnp.concatenate([table[s] for s in sites], 0)

        inner = [cat(g_self), cat(g_tin), cat(g_zin)]
        acc_ref[agg] = project(jnp.concatenate([own] * 3, 1), jnp.concatenate(inner, 0))
        t_out = cat(g_tout)
        part_ref[agg, 0] = fold(project(own_t0, t_out)).astype(BF16)
        part_ref[agg, 1] = fold(project(own_t1, t_out)).astype(BF16)
        if agg > 0:
            z = 2 * agg
            down = [hop(links_ref[z, t, minus[2]], rows_ref[2 * (z - 1) + t]) for t in range(2)]
            part_ref[agg, 2] = fold(project(own[:, :128], jnp.concatenate(down, 0))).astype(BF16)
        if agg < 3:
            z = 2 * agg + 1
            up = [hop(links_ref[z, t, plus[2]], rows_ref[2 * (z + 1) + t]) for t in range(2)]
            part_ref[agg, 3] = fold(project(own[:, 128:], jnp.concatenate(up, 0))).astype(BF16)
    part_ref[0, 2] = jnp.zeros((16, 128), BF16)
    part_ref[3, 3] = jnp.zeros((16, 128), BF16)


def across_kernel(
    off_ref,
    links_ref,
    xa_ref,
    xb_ref,
    ya_ref,
    yb_ref,
    zl_ref,
    zh_ref,
    part_ref,
    acc_ref,
    own_ref,
    out_ref,
):
    k_self, minus, plus = roles_of(off_ref)
    x_odd = lax.axis_index("xl") == 1
    y_odd = lax.axis_index("yp") == 1
    x_out = jnp.where(x_odd, plus[0], minus[0])
    x_in = jnp.where(x_odd, minus[0], plus[0])
    y_out = jnp.where(y_odd, plus[1], minus[1])
    y_in = jnp.where(y_odd, minus[1], plus[1])
    zero = jnp.zeros((16, 128), BF16)
    for agg in range(4):
        own = own_ref[agg]
        sites = sites_of(agg)

        def halo(ref, k):
            return jnp.concatenate([hop(links_ref[z, t, k], block_of(ref[z, t])) for z, t in sites], 0)

        inner = jnp.concatenate([halo(xa_ref, x_in), halo(ya_ref, y_in)], 0)
        total = acc_ref[agg] + project(jnp.concatenate([own] * 2, 1), inner)
        out_ref[agg, k_self] = fold(total).astype(BF16)
        out_ref[agg, x_out] = fold(project(own, halo(xb_ref, x_out))).astype(BF16)
        out_ref[agg, y_out] = fold(project(own, halo(yb_ref, y_out))).astype(BF16)
        out_ref[agg, x_in] = zero
        out_ref[agg, y_in] = zero
        out_ref[agg, minus[3]] = part_ref[agg, 0]
        out_ref[agg, plus[3]] = part_ref[agg, 1]
        if agg > 0:
            out_ref[agg, minus[2]] = part_ref[agg, 2]
        else:
            down = [hop(links_ref[0, t, minus[2]], block_of(zl_ref[0, t])) for t in range(2)]
            out_ref[agg, minus[2]] = fold(project(own[:, :128], jnp.concatenate(down, 0))).astype(BF16)
        if agg < 3:
            out_ref[agg, plus[2]] = part_ref[agg, 3]
        else:
            up = [hop(links_ref[7, t, plus[2]], block_of(zh_ref[0, t])) for t in range(2)]
            out_ref[agg, plus[2]] = fold(project(own[:, 128:], jnp.concatenate(up, 0))).astype(BF16)


def place_kernel(place_ref, own_ref, other_ref, out_ref, table_ref, wide_ref, buf_ref, sems):
    line = lax.axis_index("xh")
    column = lax.axis_index("xl")
    block = lax.axis_index("gz")

    for entry in range(32):
        target = place_ref[line, entry // 4, block * 4 + entry % 4]
        table_ref[target] = jnp.int32(entry)

    def gather(slot, carry):
        entry = table_ref[column * 16 + slot]
        source = 2 * (entry // 4) + entry % 2
        is_own = (entry % 4) // 2 == column
        rows = pl.ds(pl.multiple_of(slot * 16, 16), 16)
        for k in range(9):
            picked = jnp.where(is_own, own_ref[source, k].astype(F32), other_ref[source, k].astype(F32))
            wide_ref[k, rows, :] = picked
        return carry

    lax.fori_loop(0, 16, gather, 0, unroll=4)
    copies = []
    for k in range(9):
        for lane in range(16):
            buf_ref[k, :, lane * 128 : (lane + 1) * 128] = wide_ref[k, pl.ds(lane, 16, stride=16), :]
        copies.append(pltpu.make_async_copy(buf_ref.at[k], out_ref.at[k], sems.at[k]))
        copies[k].start()
    for copy in copies:
        copy.wait()


def local(links, null_vectors, offsets, place):
    own = null_vectors[0, 0]
    links = links[0, 0]
    z_low = lax.ppermute(own[7:8], "gz", shift(4, 1))
    z_high = lax.ppermute(own[0:1], "gz", shift(4, -1))
    x_inner = lax.ppermute(own, "xl", swap_inner(2))
    x_outer = lax.ppermute(own, GX, swap_outer(16))
    y_inner = lax.ppermute(own, "yp", swap_inner(2))
    y_outer = lax.ppermute(own, GY, swap_outer(16))
    vmem = pl.BlockSpec(memory_space=pltpu.VMEM)
    smem = pl.BlockSpec(memory_space=pltpu.SMEM)
    anywhere = pl.BlockSpec(memory_space=pl.ANY)
    roles = offsets.T
    part, acc, packed = pl.pallas_call(
        inside_kernel,
        out_shape=(
            jax.ShapeDtypeStruct((4, 4, 16, 128), BF16),
            jax.ShapeDtypeStruct((4, 64, 64), F32),
            jax.ShapeDtypeStruct((4, 64, 256), BF16),
        ),
        in_specs=[smem, vmem, vmem],
        out_specs=(vmem, vmem, vmem),
        scratch_shapes=[pltpu.VMEM((512, 128), F32), pltpu.VMEM((16, 64, 128), BF16)],
        compiler_params=pltpu.CompilerParams(vmem_limit_bytes=16 * 1024 * 1024),
        cost_estimate=pl.CostEstimate(flops=150_000_000, bytes_accessed=3_000_000, transcendentals=0),
        name="inside",
    )(roles, links, own)
    partial_value = pl.pallas_call(
        across_kernel,
        out_shape=jax.ShapeDtypeStruct((4, 9, 16, 128), BF16),
        in_specs=[smem] + [vmem] * 10,
        out_specs=vmem,
        compiler_params=pltpu.CompilerParams(vmem_limit_bytes=16 * 1024 * 1024),
        cost_estimate=pl.CostEstimate(flops=150_000_000, bytes_accessed=3_000_000, transcendentals=0),
        name="across",
    )(roles, links, x_inner, x_outer, y_inner, y_outer, z_low, z_high, part, acc, packed)
    parts = lax.all_to_all(partial_value, ("xl", "yp"), 0, 0, tiled=True)
    chunk = jnp.sum(parts.astype(F32), axis=0).astype(BF16)
    spread = jnp.broadcast_to(chunk[None], (16, 9, 16, 128))
    mine = lax.all_to_all(spread, GY, 0, 0, tiled=True)
    other = lax.ppermute(mine, "xl", swap_inner(2))
    placed = pl.pallas_call(
        place_kernel,
        out_shape=jax.ShapeDtypeStruct((9, 16, 2048), F32),
        in_specs=[smem, vmem, vmem],
        out_specs=anywhere,
        scratch_shapes=[
            pltpu.SMEM((32,), jnp.int32),
            pltpu.VMEM((9, 256, 128), F32),
            pltpu.VMEM((9, 16, 2048), F32),
            pltpu.SemaphoreType.DMA((9,)),
        ],
        compiler_params=pltpu.CompilerParams(vmem_limit_bytes=32 * 1024 * 1024),
        name="place",
    )(place.reshape(8, 8, 16), mine, other)
    return jnp.transpose(placed, (1, 0, 2))[None, None]


def solution(mesh):
    fine = Mesh(mesh.devices.reshape(8, 2, 2, 4, 2, 4), ("xh", "xl", "yl", "yh", "yp", "gz"))
    placed = (P(GX, GY, "gz"), P(GX, GY, "gz"), P(), P())
    return jax.shard_map(
        local,
        mesh=fine,
        in_specs=placed,
        out_specs=P(GX, "gz"),
        check_vma=False,
    )
```

```python
import jax
import jax.numpy as jnp
from jax import lax
from jax.experimental import pallas as pl
from jax.experimental.pallas import tpu as pltpu
from jax.sharding import Mesh, PartitionSpec as P

F32 = jnp.float32
BF16 = jnp.bfloat16
GX = ("xh", "xl")
GY = ("yl", "yh", "yp")


def swap_inner(count):
    return [(i, i ^ 1) for i in range(count)]


def shift(count, step):
    return [(i, (i + step) % count) for i in range(count)]


def lane_index(shape):
    return lax.broadcasted_iota(jnp.int32, shape, 1)


def block_of(vectors, signs):
    return jnp.concatenate(
        [vectors * signs, jnp.concatenate([vectors[:, 64:], vectors[:, :64]], 1)], 0
    )


def lane_signs():
    return jnp.where(lane_index((32, 128)) < 64, 1.0, -1.0).astype(BF16)


def hop(link_block, rows):
    out = lax.dot_general(link_block, rows, (((1,), (1,)), ((), ())), preferred_element_type=F32)
    return out.astype(BF16)


def project(own, stacked):
    return jnp.dot(own, stacked, preferred_element_type=F32)


def fold(result):
    first = jnp.concatenate([result[0:16], result[16:32]], 1)
    second = jnp.concatenate([result[32:48], result[48:64]], 1)
    low = lane_index((16, 128)) % 64 < 32
    return first + jnp.where(low, pltpu.roll(second, 96, 1), -pltpu.roll(second, 32, 1))


def roles_of(role_ref):
    return role_ref[8], [role_ref[axis] for axis in range(4)], [role_ref[4 + axis] for axis in range(4)]


def prepare_kernel(
    off_ref, v_ref, role_ref, low_ref, high_ref, rows_ref, own_ref, first_ref, second_ref, vf_ref
):
    k_self = jnp.int32(36)
    for place, (axis, sign) in enumerate([(a, g) for g in (-1, 1) for a in range(4)]):
        index = jnp.int32(0)
        for k in range(9):
            index = index + jnp.where(off_ref[axis, k] == sign, k, 0).astype(jnp.int32)
        role_ref[place] = index
        k_self = k_self - index
    role_ref[8] = k_self
    low_ref[0] = v_ref[0]
    high_ref[0] = v_ref[7]
    signs = lane_signs()
    for z in range(8):
        for t in range(2):
            vf_ref[pl.ds((2 * z + t) * 32, 32), :] = v_ref[z, t].astype(F32)
            rows_ref[2 * z + t] = block_of(v_ref[z, t], signs)
    low = lane_index((16, 128)) < 64
    low_own = lane_index((64, 128)) < 64
    for z in range(8):
        base = z * 64
        quarter = []
        for first in range(2):
            left = vf_ref[pl.ds(base + first, 16, stride=2), :]
            right = vf_ref[pl.ds(base + 32 + first, 16, stride=2), :]
            quarter.append(
                (
                    jnp.where(low, left, pltpu.roll(right, 64, 1)),
                    jnp.where(low, pltpu.roll(left, 64, 1), right),
                )
            )
        half = jnp.concatenate([quarter[0][0], quarter[1][0], quarter[0][1], quarter[1][1]], 0)
        lanes = slice((z % 2) * 128, (z % 2) * 128 + 128)
        own_ref[z // 2, :, lanes] = half.astype(BF16)
        first_ref[z // 2, :, lanes] = jnp.where(low_own, half, 0.0).astype(BF16)
        second_ref[z // 2, :, lanes] = jnp.where(low_own, 0.0, half).astype(BF16)


def inside_kernel(
    off_ref, links_ref, rows_ref, own_ref, first_ref, second_ref, part_ref, acc_ref, hop_ref
):
    k_self, minus, plus = roles_of(off_ref)
    for z in range(8):
        agg = z // 2
        for t in range(2):
            k_tin = plus[3] if t == 1 else minus[3]
            k_tout = minus[3] if t == 1 else plus[3]
            k_zin = minus[2] if z % 2 == 0 else plus[2]
            target = z - 1 if z % 2 == 0 else z + 1
            stack = [
                links_ref[z, t, k_self],
                links_ref[z, 1 - t, k_tin],
                links_ref[z ^ 1, t, k_zin],
                links_ref[z, 1 - t, k_tout],
            ]
            if 0 <= target <= 7:
                k_back = plus[2] if z % 2 == 0 else minus[2]
                stack.append(links_ref[target, t, k_back])
            res = hop(jnp.concatenate(stack, 0), rows_ref[2 * z + t])
            here = (2 * (z % 2) + t) * 64
            side = (2 * (z % 2) + 1 - t) * 64
            across = (2 * (1 - z % 2) + t) * 64
            hop_ref[agg, here : here + 64] = res[0:64]
            hop_ref[agg, 256 + side : 256 + side + 64] = res[64:128]
            hop_ref[agg, 512 + across : 512 + across + 64] = res[128:192]
            hop_ref[agg, 768 + side : 768 + side + 64] = res[192:256]
            if 0 <= target <= 7:
                row = 1024 + (2 * (target % 2) + t) * 64
                hop_ref[target // 2, row : row + 64] = res[256:320]
    for agg in range(4):
        own = own_ref[agg]
        acc_ref[agg] = project(jnp.concatenate([own] * 3, 1), hop_ref[agg, 0:768])
        part_ref[agg, 0] = fold(project(first_ref[agg], hop_ref[agg, 768:1024])).astype(BF16)
        part_ref[agg, 1] = fold(project(second_ref[agg], hop_ref[agg, 768:1024])).astype(BF16)
        if agg > 0:
            part_ref[agg, 2] = fold(project(own[:, :128], hop_ref[agg, 1024:1152])).astype(BF16)
        if agg < 3:
            part_ref[agg, 3] = fold(project(own[:, 128:], hop_ref[agg, 1152:1280])).astype(BF16)
    part_ref[0, 2] = jnp.zeros((16, 128), BF16)
    part_ref[3, 3] = jnp.zeros((16, 128), BF16)


def across_kernel(
    role_ref,
    links_ref,
    xl_ref,
    xh_ref,
    yl_ref,
    yh_ref,
    zl_ref,
    zh_ref,
    part_ref,
    acc_ref,
    own_ref,
    out_ref,
    rows_ref,
    hop_ref,
):
    k_self, minus, plus = roles_of(role_ref)
    x_odd = lax.axis_index("xl")
    y_odd = lax.axis_index("yp")
    x_out = jnp.where(x_odd == 1, plus[0], minus[0])
    x_in = jnp.where(x_odd == 1, minus[0], plus[0])
    y_out = jnp.where(y_odd == 1, plus[1], minus[1])
    y_in = jnp.where(y_odd == 1, minus[1], plus[1])
    x_base = pl.multiple_of(512 * x_odd, 256)
    y_base = pl.multiple_of(512 * y_odd, 256)
    zero = jnp.zeros((16, 128), BF16)
    signs = lane_signs()
    sides = (
        (xl_ref, minus[0], 512 - x_base),
        (xh_ref, plus[0], x_base),
        (yl_ref, minus[1], 768 - y_base),
        (yh_ref, plus[1], 256 + y_base),
    )
    for t in range(2):
        rows_ref[64 + t] = block_of(zl_ref[0, t], signs)
        rows_ref[66 + t] = block_of(zh_ref[0, t], signs)
    for z in range(8):
        for t in range(2):
            for role, (ref, _, _) in enumerate(sides):
                rows_ref[role * 16 + 2 * z + t] = block_of(ref[z, t], signs)
    for t in range(2):
        hop_ref[0, 1024 + t * 64 : 1088 + t * 64] = hop(links_ref[0, t, minus[2]], rows_ref[64 + t])
        hop_ref[3, 1024 + t * 64 : 1088 + t * 64] = hop(links_ref[7, t, plus[2]], rows_ref[66 + t])
    for z in range(8):
        for t in range(2):
            for role, (_, k, base) in enumerate(sides):
                row = pl.multiple_of(base + (2 * (z % 2) + t) * 64, 64)
                res = hop(links_ref[z, t, k], rows_ref[role * 16 + 2 * z + t])
                hop_ref[z // 2, pl.ds(row, 64)] = res
    for agg in range(4):
        own = own_ref[agg]
        total = acc_ref[agg] + project(jnp.concatenate([own] * 2, 1), hop_ref[agg, 0:512])
        out_ref[agg, k_self] = fold(total).astype(BF16)
        out_ref[agg, x_out] = fold(project(own, hop_ref[agg, 512:768])).astype(BF16)
        out_ref[agg, y_out] = fold(project(own, hop_ref[agg, 768:1024])).astype(BF16)
        out_ref[agg, x_in] = zero
        out_ref[agg, y_in] = zero
        out_ref[agg, minus[3]] = part_ref[agg, 0]
        out_ref[agg, plus[3]] = part_ref[agg, 1]
        if agg > 0:
            out_ref[agg, minus[2]] = part_ref[agg, 2]
        else:
            out_ref[agg, minus[2]] = fold(project(own[:, :128], hop_ref[0, 1024:1152])).astype(BF16)
        if agg < 3:
            out_ref[agg, plus[2]] = part_ref[agg, 3]
        else:
            out_ref[agg, plus[2]] = fold(project(own[:, 128:], hop_ref[3, 1024:1152])).astype(BF16)


def place_kernel(place_ref, own_ref, other_ref, out_ref, table_ref, wide_ref, buf_ref, sems):
    line = lax.axis_index("xh")
    column = lax.axis_index("xl")
    block = lax.axis_index("gz")

    for entry in range(32):
        target = place_ref[line, entry // 4, block * 4 + entry % 4]
        table_ref[target] = jnp.int32(entry)

    def gather(slot, carry):
        entry = table_ref[column * 16 + slot]
        source = 2 * (entry // 4) + entry % 2
        is_own = (entry % 4) // 2 == column
        rows = pl.ds(pl.multiple_of(slot * 16, 16), 16)
        for k in range(9):
            picked = jnp.where(is_own, own_ref[source, k].astype(F32), other_ref[source, k].astype(F32))
            wide_ref[k, rows, :] = picked
        return carry

    lax.fori_loop(0, 16, gather, 0, unroll=4)
    copies = []
    for k in range(9):
        for lane in range(16):
            buf_ref[k, :, lane * 128 : (lane + 1) * 128] = wide_ref[k, pl.ds(lane, 16, stride=16), :]
        copies.append(pltpu.make_async_copy(buf_ref.at[k], out_ref.at[k], sems.at[k]))
        copies[k].start()
    for copy in copies:
        copy.wait()


def local(links, null_vectors, offsets, place):
    own = null_vectors[0, 0]
    links = links[0, 0]
    vmem = pl.BlockSpec(memory_space=pltpu.VMEM)
    smem = pl.BlockSpec(memory_space=pltpu.SMEM)
    anywhere = pl.BlockSpec(memory_space=pl.ANY)
    role_table, slab_low, slab_high, rows, packed, packed_first, packed_second = pl.pallas_call(
        prepare_kernel,
        out_shape=(jax.ShapeDtypeStruct((9,), jnp.int32),)
        + (jax.ShapeDtypeStruct((1, 2, 32, 128), BF16),) * 2
        + (jax.ShapeDtypeStruct((16, 64, 128), BF16),)
        + (jax.ShapeDtypeStruct((4, 64, 256), BF16),) * 3,
        in_specs=[smem, vmem],
        out_specs=(smem,) + (vmem,) * 6,
        scratch_shapes=[pltpu.VMEM((512, 128), F32)],
        compiler_params=pltpu.CompilerParams(vmem_limit_bytes=16 * 1024 * 1024),
        cost_estimate=pl.CostEstimate(
            flops=2_000_000_000, bytes_accessed=10_000_000, transcendentals=0
        ),
        name="prepare",
    )(offsets.T, own)
    z_low = lax.ppermute(slab_high, "gz", shift(4, 1))
    z_high = lax.ppermute(slab_low, "gz", shift(4, -1))
    y_low = lax.ppermute(own, GY, shift(16, 1))
    y_high = lax.ppermute(own, GY, shift(16, -1))
    x_low = lax.ppermute(own, GX, shift(16, 1))
    x_high = lax.ppermute(own, GX, shift(16, -1))
    part, acc = pl.pallas_call(
        inside_kernel,
        out_shape=(
            jax.ShapeDtypeStruct((4, 4, 16, 128), BF16),
            jax.ShapeDtypeStruct((4, 64, 64), F32),
        ),
        in_specs=[smem] + [vmem] * 5,
        out_specs=(vmem, vmem),
        scratch_shapes=[pltpu.VMEM((4, 1280, 64), BF16)],
        compiler_params=pltpu.CompilerParams(vmem_limit_bytes=16 * 1024 * 1024),
        cost_estimate=pl.CostEstimate(flops=150_000_000, bytes_accessed=3_000_000, transcendentals=0),
        name="inside",
    )(role_table, links, rows, packed, packed_first, packed_second)
    partial_value = pl.pallas_call(
        across_kernel,
        out_shape=jax.ShapeDtypeStruct((4, 9, 16, 128), BF16),
        in_specs=[smem] + [vmem] * 10,
        out_specs=vmem,
        scratch_shapes=[pltpu.VMEM((68, 64, 128), BF16), pltpu.VMEM((4, 1152, 64), BF16)],
        compiler_params=pltpu.CompilerParams(vmem_limit_bytes=16 * 1024 * 1024),
        cost_estimate=pl.CostEstimate(flops=150_000_000, bytes_accessed=3_000_000, transcendentals=0),
        name="across",
    )(role_table, links, x_low, x_high, y_low, y_high, z_low, z_high, part, acc, packed)
    parts = lax.all_to_all(partial_value, ("xl", "yp"), 0, 0, tiled=True)
    chunk = jnp.sum(parts.astype(F32), axis=0).astype(BF16)
    spread = jnp.broadcast_to(chunk[None], (16, 9, 16, 128))
    mine = lax.all_to_all(spread, GY, 0, 0, tiled=True)
    other = lax.ppermute(mine, "xl", swap_inner(2))
    placed = pl.pallas_call(
        place_kernel,
        out_shape=jax.ShapeDtypeStruct((9, 16, 2048), F32),
        in_specs=[smem, vmem, vmem],
        out_specs=anywhere,
        scratch_shapes=[
            pltpu.SMEM((32,), jnp.int32),
            pltpu.VMEM((9, 256, 128), F32),
            pltpu.VMEM((9, 16, 2048), F32),
            pltpu.SemaphoreType.DMA((9,)),
        ],
        compiler_params=pltpu.CompilerParams(vmem_limit_bytes=32 * 1024 * 1024),
        name="place",
    )(place.reshape(8, 8, 16), mine, other)
    return jnp.transpose(placed, (1, 0, 2))[None, None]


def solution(mesh):
    fine = Mesh(mesh.devices.reshape(8, 2, 2, 4, 2, 4), ("xh", "xl", "yl", "yh", "yp", "gz"))
    placed = (P(GX, GY, "gz"), P(GX, GY, "gz"), P(), P())
    return jax.shard_map(
        local,
        mesh=fine,
        in_specs=placed,
        out_specs=P(GX, "gz"),
        check_vma=False,
    )
```

```python
import jax
import jax.numpy as jnp
from jax import lax
from jax.experimental import pallas as pl
from jax.experimental.pallas import tpu as pltpu
from jax.sharding import Mesh, PartitionSpec as P

F32 = jnp.float32
BF16 = jnp.bfloat16
GX = ("xh", "xl")
GY = ("yl", "yh", "yp")


def swap_inner(count):
    return [(i, i ^ 1) for i in range(count)]


def shift(count, step):
    return [(i, (i + step) % count) for i in range(count)]


def lane_index(shape):
    return lax.broadcasted_iota(jnp.int32, shape, 1)


def block_of(vectors, signs):
    return jnp.concatenate(
        [vectors * signs, jnp.concatenate([vectors[:, 64:], vectors[:, :64]], 1)], 0
    )


def lane_signs():
    return jnp.where(lane_index((32, 128)) < 64, 1.0, -1.0).astype(BF16)


def hop(link_block, rows):
    out = lax.dot_general(link_block, rows, (((1,), (1,)), ((), ())), preferred_element_type=F32)
    return out.astype(BF16)


def project(own, stacked):
    return jnp.dot(own, stacked, preferred_element_type=F32)


def fold(result):
    first = jnp.concatenate([result[0:16], result[16:32]], 1)
    second = jnp.concatenate([result[32:48], result[48:64]], 1)
    low = lane_index((16, 128)) % 64 < 32
    return first + jnp.where(low, pltpu.roll(second, 96, 1), -pltpu.roll(second, 32, 1))


def roles_of(role_ref):
    return role_ref[8], [role_ref[axis] for axis in range(4)], [role_ref[4 + axis] for axis in range(4)]


def prepare_kernel(v_ref, slab_ref, rows_ref, own_ref, vf_ref):
    after = (lax.axis_index("gz") + 1) % 4
    for step in range(1, 4):
        slab_ref[(after + step) % 4] = v_ref[0]
    slab_ref[after] = v_ref[7]
    signs = lane_signs()
    for z in range(8):
        for t in range(2):
            vf_ref[pl.ds((2 * z + t) * 32, 32), :] = v_ref[z, t].astype(F32)
            rows_ref[2 * z + t] = block_of(v_ref[z, t], signs)
    low = lane_index((16, 128)) < 64
    for z in range(8):
        base = z * 64
        quarter = []
        for first in range(2):
            left = vf_ref[pl.ds(base + first, 16, stride=2), :]
            right = vf_ref[pl.ds(base + 32 + first, 16, stride=2), :]
            quarter.append(
                (
                    jnp.where(low, left, pltpu.roll(right, 64, 1)),
                    jnp.where(low, pltpu.roll(left, 64, 1), right),
                )
            )
        half = jnp.concatenate([quarter[0][0], quarter[1][0], quarter[0][1], quarter[1][1]], 0)
        lanes = slice((z % 2) * 128, (z % 2) * 128 + 128)
        own_ref[z // 2, :, lanes] = half.astype(BF16)


def inside_kernel(
    off_ref,
    links_ref,
    rows_ref,
    own_ref,
    part_ref,
    acc_ref,
    role_ref,
    hop_ref,
):
    k_self = jnp.int32(36)
    found = []
    for place, (axis, sign) in enumerate([(a, g) for g in (-1, 1) for a in range(4)]):
        index = jnp.int32(0)
        for k in range(9):
            index = index + jnp.where(off_ref[axis, k] == sign, k, 0).astype(jnp.int32)
        role_ref[place] = index
        found.append(index)
        k_self = k_self - index
    role_ref[8] = k_self
    minus, plus = found[:4], found[4:]
    for z in range(8):
        agg = z // 2
        for t in range(2):
            k_tin = plus[3] if t == 1 else minus[3]
            k_tout = minus[3] if t == 1 else plus[3]
            k_zin = minus[2] if z % 2 == 0 else plus[2]
            target = z - 1 if z % 2 == 0 else z + 1
            stack = [
                links_ref[z, t, k_self],
                links_ref[z, 1 - t, k_tin],
                links_ref[z ^ 1, t, k_zin],
                links_ref[z, 1 - t, k_tout],
            ]
            if 0 <= target <= 7:
                k_back = plus[2] if z % 2 == 0 else minus[2]
                stack.append(links_ref[target, t, k_back])
            res = hop(jnp.concatenate(stack, 0), rows_ref[2 * z + t])
            here = (2 * (z % 2) + t) * 64
            side = (2 * (z % 2) + 1 - t) * 64
            across = (2 * (1 - z % 2) + t) * 64
            hop_ref[agg, here : here + 64] = res[0:64]
            hop_ref[agg, 256 + side : 256 + side + 64] = res[64:128]
            hop_ref[agg, 512 + across : 512 + across + 64] = res[128:192]
            hop_ref[agg, 768 + side : 768 + side + 64] = res[192:256]
            if 0 <= target <= 7:
                row = 1024 + (2 * (target % 2) + t) * 64
                hop_ref[target // 2, row : row + 64] = res[256:320]
    first = jnp.where(lane_index((64, 256)) % 128 < 64, 1.0, 0.0).astype(BF16)
    second = jnp.where(lane_index((64, 256)) % 128 < 64, 0.0, 1.0).astype(BF16)
    for agg in range(4):
        own = own_ref[agg]
        acc_ref[agg] = project(jnp.concatenate([own] * 3, 1), hop_ref[agg, 0:768])
        part_ref[agg, 0] = fold(project(own * first, hop_ref[agg, 768:1024])).astype(BF16)
        part_ref[agg, 1] = fold(project(own * second, hop_ref[agg, 768:1024])).astype(BF16)
        if agg > 0:
            part_ref[agg, 2] = fold(project(own[:, :128], hop_ref[agg, 1024:1152])).astype(BF16)
        if agg < 3:
            part_ref[agg, 3] = fold(project(own[:, 128:], hop_ref[agg, 1152:1280])).astype(BF16)
    part_ref[0, 2] = jnp.zeros((16, 128), BF16)
    part_ref[3, 3] = jnp.zeros((16, 128), BF16)


def across_kernel(
    role_ref,
    links_ref,
    xl_ref,
    xh_ref,
    yl_ref,
    yh_ref,
    z_ref,
    part_ref,
    acc_ref,
    own_ref,
    out_ref,
    rows_ref,
    hop_ref,
):
    k_self, minus, plus = roles_of(role_ref)
    x_odd = lax.axis_index("xl")
    y_odd = lax.axis_index("yp")
    block = lax.axis_index("gz")
    x_out = jnp.where(x_odd == 1, plus[0], minus[0])
    x_in = jnp.where(x_odd == 1, minus[0], plus[0])
    y_out = jnp.where(y_odd == 1, plus[1], minus[1])
    y_in = jnp.where(y_odd == 1, minus[1], plus[1])
    x_base = pl.multiple_of(512 * x_odd, 256)
    y_base = pl.multiple_of(512 * y_odd, 256)
    zero = jnp.zeros((16, 128), BF16)
    signs = lane_signs()
    sides = (
        (xl_ref, minus[0], 512 - x_base),
        (xh_ref, plus[0], x_base),
        (yl_ref, minus[1], 768 - y_base),
        (yh_ref, plus[1], 256 + y_base),
    )
    for t in range(2):
        rows_ref[64 + t] = block_of(z_ref[(block + 3) % 4, t], signs)
        rows_ref[66 + t] = block_of(z_ref[(block + 1) % 4, t], signs)
    for z in range(8):
        for t in range(2):
            for role, (ref, _, _) in enumerate(sides):
                rows_ref[role * 16 + 2 * z + t] = block_of(ref[z, t], signs)
    for t in range(2):
        hop_ref[0, 1024 + t * 64 : 1088 + t * 64] = hop(links_ref[0, t, minus[2]], rows_ref[64 + t])
        hop_ref[3, 1024 + t * 64 : 1088 + t * 64] = hop(links_ref[7, t, plus[2]], rows_ref[66 + t])
    for z in range(8):
        for t in range(2):
            for role, (_, k, base) in enumerate(sides):
                row = pl.multiple_of(base + (2 * (z % 2) + t) * 64, 64)
                res = hop(links_ref[z, t, k], rows_ref[role * 16 + 2 * z + t])
                hop_ref[z // 2, pl.ds(row, 64)] = res
    for agg in range(4):
        own = own_ref[agg]
        total = acc_ref[agg] + project(jnp.concatenate([own] * 2, 1), hop_ref[agg, 0:512])
        out_ref[agg, k_self] = fold(total).astype(BF16)
        out_ref[agg, x_out] = fold(project(own, hop_ref[agg, 512:768])).astype(BF16)
        out_ref[agg, y_out] = fold(project(own, hop_ref[agg, 768:1024])).astype(BF16)
        out_ref[agg, x_in] = zero
        out_ref[agg, y_in] = zero
        out_ref[agg, minus[3]] = part_ref[agg, 0]
        out_ref[agg, plus[3]] = part_ref[agg, 1]
        if agg > 0:
            out_ref[agg, minus[2]] = part_ref[agg, 2]
        else:
            out_ref[agg, minus[2]] = fold(project(own[:, :128], hop_ref[0, 1024:1152])).astype(BF16)
        if agg < 3:
            out_ref[agg, plus[2]] = part_ref[agg, 3]
        else:
            out_ref[agg, plus[2]] = fold(project(own[:, 128:], hop_ref[3, 1024:1152])).astype(BF16)


def gather_kernel(place_ref, own_ref, wide_ref, table_ref):
    line = lax.axis_index("xh")
    column = lax.axis_index("xl")
    block = lax.axis_index("gz")
    for entry in range(32):
        table_ref[place_ref[line, entry // 4, block * 4 + entry % 4]] = jnp.int32(entry)

    def gather(slot, carry):
        entry = table_ref[column * 16 + slot]
        source = 2 * (entry // 4) + entry % 2
        rows = pl.ds(pl.multiple_of(slot * 16, 16), 16)
        for k in range(9):
            wide_ref[k, rows, :] = own_ref[source, k].astype(F32)
        return carry

    lax.fori_loop(0, 16, gather, 0, unroll=4)


def place_kernel(table_ref, other_ref, wide_ref, out_ref, work_ref, buf_ref, sems):
    column = lax.axis_index("xl")

    def gather(slot, carry):
        entry = table_ref[column * 16 + slot]
        source = 2 * (entry // 4) + entry % 2
        is_own = (entry % 4) // 2 == column
        rows = pl.ds(pl.multiple_of(slot * 16, 16), 16)
        for k in range(9):
            work_ref[k, rows, :] = jnp.where(is_own, wide_ref[k, rows, :], other_ref[source, k].astype(F32))
        return carry

    lax.fori_loop(0, 16, gather, 0, unroll=4)
    copies = []
    for k in range(9):
        for lane in range(16):
            buf_ref[k, :, lane * 128 : (lane + 1) * 128] = work_ref[k, pl.ds(lane, 16, stride=16), :]
        copies.append(pltpu.make_async_copy(buf_ref.at[k], out_ref.at[k], sems.at[k]))
        copies[k].start()
    for copy in copies:
        copy.wait()


def local(links, null_vectors, offsets, place):
    own = null_vectors[0, 0]
    links = links[0, 0]
    vmem = pl.BlockSpec(memory_space=pltpu.VMEM)
    smem = pl.BlockSpec(memory_space=pltpu.SMEM)
    anywhere = pl.BlockSpec(memory_space=pl.ANY)
    slabs, rows, packed = pl.pallas_call(
        prepare_kernel,
        out_shape=(jax.ShapeDtypeStruct((4, 2, 32, 128), BF16),)
        + (jax.ShapeDtypeStruct((16, 64, 128), BF16),)
        + (jax.ShapeDtypeStruct((4, 64, 256), BF16),),
        in_specs=[vmem],
        out_specs=(vmem,) * 3,
        scratch_shapes=[pltpu.VMEM((512, 128), F32)],
        compiler_params=pltpu.CompilerParams(vmem_limit_bytes=16 * 1024 * 1024),
        cost_estimate=pl.CostEstimate(
            flops=2_000_000_000, bytes_accessed=10_000_000, transcendentals=0
        ),
        name="prepare",
    )(own)
    z_slabs = lax.all_to_all(slabs, "gz", 0, 0, tiled=True)
    y_low = lax.ppermute(own, GY, shift(16, 1))
    y_high = lax.ppermute(own, GY, shift(16, -1))
    x_low = lax.ppermute(own, GX, shift(16, 1))
    x_high = lax.ppermute(own, GX, shift(16, -1))
    part, acc, role_table = pl.pallas_call(
        inside_kernel,
        out_shape=(
            jax.ShapeDtypeStruct((4, 4, 16, 128), BF16),
            jax.ShapeDtypeStruct((4, 64, 64), F32),
            jax.ShapeDtypeStruct((9,), jnp.int32),
        ),
        in_specs=[smem] + [vmem] * 3,
        out_specs=(vmem, vmem, smem),
        scratch_shapes=[pltpu.VMEM((4, 1280, 64), BF16)],
        compiler_params=pltpu.CompilerParams(vmem_limit_bytes=16 * 1024 * 1024),
        cost_estimate=pl.CostEstimate(flops=150_000_000, bytes_accessed=3_000_000, transcendentals=0),
        name="inside",
    )(offsets.T, links, rows, packed)
    partial_value = pl.pallas_call(
        across_kernel,
        out_shape=jax.ShapeDtypeStruct((4, 9, 16, 128), BF16),
        in_specs=[smem] + [vmem] * 9,
        out_specs=vmem,
        scratch_shapes=[pltpu.VMEM((68, 64, 128), BF16), pltpu.VMEM((4, 1152, 64), BF16)],
        compiler_params=pltpu.CompilerParams(vmem_limit_bytes=16 * 1024 * 1024),
        cost_estimate=pl.CostEstimate(flops=150_000_000, bytes_accessed=3_000_000, transcendentals=0),
        name="across",
    )(role_table, links, x_low, x_high, y_low, y_high, z_slabs, part, acc, packed)
    parts = lax.all_to_all(partial_value, ("xl", "yp"), 0, 0, tiled=True)
    chunk = jnp.sum(parts.astype(F32), axis=0).astype(BF16)
    spread = jnp.broadcast_to(chunk[None], (16, 9, 16, 128))
    mine = lax.all_to_all(spread, GY, 0, 0, tiled=True)
    other = lax.ppermute(mine, "xl", swap_inner(2))
    wide, table = pl.pallas_call(
        gather_kernel,
        out_shape=(
            jax.ShapeDtypeStruct((9, 256, 128), F32),
            jax.ShapeDtypeStruct((32,), jnp.int32),
        ),
        in_specs=[smem, vmem],
        out_specs=(vmem, smem),
        compiler_params=pltpu.CompilerParams(vmem_limit_bytes=16 * 1024 * 1024),
        cost_estimate=pl.CostEstimate(flops=1_000_000, bytes_accessed=3_000_000, transcendentals=0),
        name="gather",
    )(place.reshape(8, 8, 16), mine)
    placed = pl.pallas_call(
        place_kernel,
        out_shape=jax.ShapeDtypeStruct((9, 16, 2048), F32),
        in_specs=[smem, vmem, vmem],
        out_specs=anywhere,
        scratch_shapes=[
            pltpu.VMEM((9, 256, 128), F32),
            pltpu.VMEM((9, 16, 2048), F32),
            pltpu.SemaphoreType.DMA((9,)),
        ],
        compiler_params=pltpu.CompilerParams(vmem_limit_bytes=32 * 1024 * 1024),
        name="place",
    )(table, other, wide)
    return jnp.transpose(placed, (1, 0, 2))[None, None]


def solution(mesh):
    fine = Mesh(mesh.devices.reshape(8, 2, 2, 4, 2, 4), ("xh", "xl", "yl", "yh", "yp", "gz"))
    placed = (P(GX, GY, "gz"), P(GX, GY, "gz"), P(), P())
    return jax.shard_map(
        local,
        mesh=fine,
        in_specs=placed,
        out_specs=P(GX, "gz"),
        check_vma=False,
    )
```

```python
import jax
import jax.numpy as jnp
from jax import lax
from jax.experimental import pallas as pl
from jax.experimental.pallas import tpu as pltpu
from jax.sharding import Mesh, PartitionSpec as P

F32 = jnp.float32
BF16 = jnp.bfloat16
GX = ("xh", "xl")
GY = ("yl", "yh", "yp")


def swap_inner(count):
    return [(i, i ^ 1) for i in range(count)]


def shift(count, step):
    return [(i, (i + step) % count) for i in range(count)]


def lane_index(shape):
    return lax.broadcasted_iota(jnp.int32, shape, 1)


def block_of(vectors, signs):
    return jnp.concatenate(
        [vectors * signs, jnp.concatenate([vectors[:, 64:], vectors[:, :64]], 1)], 0
    )


def lane_signs():
    return jnp.where(lane_index((32, 128)) < 64, 1.0, -1.0).astype(BF16)


def hop(link_block, rows):
    out = lax.dot_general(link_block, rows, (((1,), (1,)), ((), ())), preferred_element_type=F32)
    return out.astype(BF16)


def project(own, stacked):
    return jnp.dot(own, stacked, preferred_element_type=F32)


def fold(result):
    first = jnp.concatenate([result[0:16], result[16:32]], 1)
    second = jnp.concatenate([result[32:48], result[48:64]], 1)
    low = lane_index((16, 128)) % 64 < 32
    return first + jnp.where(low, pltpu.roll(second, 96, 1), -pltpu.roll(second, 32, 1))


def roles_of(role_ref):
    return role_ref[8], [role_ref[axis] for axis in range(4)], [role_ref[4 + axis] for axis in range(4)]


def slab_kernel(first_ref, last_ref, slab_ref):
    after = (lax.axis_index("gz") + 1) % 4
    for step in range(1, 4):
        slab_ref[(after + step) % 4] = first_ref[0]
    slab_ref[after] = last_ref[0]


def prepare_kernel(v_ref, rows_ref, own_ref, vf_ref):
    signs = lane_signs()
    for z in range(8):
        for t in range(2):
            vf_ref[pl.ds((2 * z + t) * 32, 32), :] = v_ref[z, t].astype(F32)
            rows_ref[2 * z + t] = block_of(v_ref[z, t], signs)
    low = lane_index((16, 128)) < 64
    for z in range(8):
        base = z * 64
        quarter = []
        for first in range(2):
            left = vf_ref[pl.ds(base + first, 16, stride=2), :]
            right = vf_ref[pl.ds(base + 32 + first, 16, stride=2), :]
            quarter.append(
                (
                    jnp.where(low, left, pltpu.roll(right, 64, 1)),
                    jnp.where(low, pltpu.roll(left, 64, 1), right),
                )
            )
        half = jnp.concatenate([quarter[0][0], quarter[1][0], quarter[0][1], quarter[1][1]], 0)
        lanes = slice((z % 2) * 128, (z % 2) * 128 + 128)
        own_ref[z // 2, :, lanes] = half.astype(BF16)


def inside_kernel(
    off_ref,
    links_ref,
    rows_ref,
    own_ref,
    part_ref,
    acc_ref,
    role_ref,
    hop_ref,
):
    k_self = jnp.int32(36)
    found = []
    for place, (axis, sign) in enumerate([(a, g) for g in (-1, 1) for a in range(4)]):
        index = jnp.int32(0)
        for k in range(9):
            index = index + jnp.where(off_ref[axis, k] == sign, k, 0).astype(jnp.int32)
        role_ref[place] = index
        found.append(index)
        k_self = k_self - index
    role_ref[8] = k_self
    minus, plus = found[:4], found[4:]
    for z in range(8):
        agg = z // 2
        for t in range(2):
            k_tin = plus[3] if t == 1 else minus[3]
            k_tout = minus[3] if t == 1 else plus[3]
            k_zin = minus[2] if z % 2 == 0 else plus[2]
            target = z - 1 if z % 2 == 0 else z + 1
            stack = [
                links_ref[z, t, k_self],
                links_ref[z, 1 - t, k_tin],
                links_ref[z ^ 1, t, k_zin],
                links_ref[z, 1 - t, k_tout],
            ]
            if 0 <= target <= 7:
                k_back = plus[2] if z % 2 == 0 else minus[2]
                stack.append(links_ref[target, t, k_back])
            res = hop(jnp.concatenate(stack, 0), rows_ref[2 * z + t])
            here = (2 * (z % 2) + t) * 64
            side = (2 * (z % 2) + 1 - t) * 64
            across = (2 * (1 - z % 2) + t) * 64
            hop_ref[agg, here : here + 64] = res[0:64]
            hop_ref[agg, 256 + side : 256 + side + 64] = res[64:128]
            hop_ref[agg, 512 + across : 512 + across + 64] = res[128:192]
            hop_ref[agg, 768 + side : 768 + side + 64] = res[192:256]
            if 0 <= target <= 7:
                row = 1024 + (2 * (target % 2) + t) * 64
                hop_ref[target // 2, row : row + 64] = res[256:320]
    first = jnp.where(lane_index((64, 256)) % 128 < 64, 1.0, 0.0).astype(BF16)
    second = jnp.where(lane_index((64, 256)) % 128 < 64, 0.0, 1.0).astype(BF16)
    for agg in range(4):
        own = own_ref[agg]
        acc_ref[agg] = project(jnp.concatenate([own] * 3, 1), hop_ref[agg, 0:768])
        part_ref[agg, 0] = fold(project(own * first, hop_ref[agg, 768:1024])).astype(BF16)
        part_ref[agg, 1] = fold(project(own * second, hop_ref[agg, 768:1024])).astype(BF16)
        if agg > 0:
            part_ref[agg, 2] = fold(project(own[:, :128], hop_ref[agg, 1024:1152])).astype(BF16)
        if agg < 3:
            part_ref[agg, 3] = fold(project(own[:, 128:], hop_ref[agg, 1152:1280])).astype(BF16)
    part_ref[0, 2] = jnp.zeros((16, 128), BF16)
    part_ref[3, 3] = jnp.zeros((16, 128), BF16)


def across_kernel(
    role_ref,
    links_ref,
    xl_ref,
    xh_ref,
    yl_ref,
    yh_ref,
    z_ref,
    part_ref,
    acc_ref,
    own_ref,
    out_ref,
    rows_ref,
    hop_ref,
):
    k_self, minus, plus = roles_of(role_ref)
    x_odd = lax.axis_index("xl")
    y_odd = lax.axis_index("yp")
    block = lax.axis_index("gz")
    x_out = jnp.where(x_odd == 1, plus[0], minus[0])
    x_in = jnp.where(x_odd == 1, minus[0], plus[0])
    y_out = jnp.where(y_odd == 1, plus[1], minus[1])
    y_in = jnp.where(y_odd == 1, minus[1], plus[1])
    x_base = pl.multiple_of(512 * x_odd, 256)
    y_base = pl.multiple_of(512 * y_odd, 256)
    zero = jnp.zeros((16, 128), BF16)
    signs = lane_signs()
    sides = (
        (xl_ref, minus[0], 512 - x_base),
        (xh_ref, plus[0], x_base),
        (yl_ref, minus[1], 768 - y_base),
        (yh_ref, plus[1], 256 + y_base),
    )
    for t in range(2):
        rows_ref[64 + t] = block_of(z_ref[(block + 3) % 4, t], signs)
        rows_ref[66 + t] = block_of(z_ref[(block + 1) % 4, t], signs)
    for z in range(8):
        for t in range(2):
            for role, (ref, _, _) in enumerate(sides):
                rows_ref[role * 16 + 2 * z + t] = block_of(ref[z, t], signs)
    for t in range(2):
        hop_ref[0, 1024 + t * 64 : 1088 + t * 64] = hop(links_ref[0, t, minus[2]], rows_ref[64 + t])
        hop_ref[3, 1024 + t * 64 : 1088 + t * 64] = hop(links_ref[7, t, plus[2]], rows_ref[66 + t])
    for z in range(8):
        for t in range(2):
            for role, (_, k, base) in enumerate(sides):
                row = pl.multiple_of(base + (2 * (z % 2) + t) * 64, 64)
                res = hop(links_ref[z, t, k], rows_ref[role * 16 + 2 * z + t])
                hop_ref[z // 2, pl.ds(row, 64)] = res
    for agg in range(4):
        own = own_ref[agg]
        total = acc_ref[agg] + project(jnp.concatenate([own] * 2, 1), hop_ref[agg, 0:512])
        out_ref[agg, k_self] = fold(total).astype(BF16)
        out_ref[agg, x_out] = fold(project(own, hop_ref[agg, 512:768])).astype(BF16)
        out_ref[agg, y_out] = fold(project(own, hop_ref[agg, 768:1024])).astype(BF16)
        out_ref[agg, x_in] = zero
        out_ref[agg, y_in] = zero
        out_ref[agg, minus[3]] = part_ref[agg, 0]
        out_ref[agg, plus[3]] = part_ref[agg, 1]
        if agg > 0:
            out_ref[agg, minus[2]] = part_ref[agg, 2]
        else:
            out_ref[agg, minus[2]] = fold(project(own[:, :128], hop_ref[0, 1024:1152])).astype(BF16)
        if agg < 3:
            out_ref[agg, plus[2]] = part_ref[agg, 3]
        else:
            out_ref[agg, plus[2]] = fold(project(own[:, 128:], hop_ref[3, 1024:1152])).astype(BF16)


def gather_kernel(place_ref, own_ref, wide_ref, table_ref):
    line = lax.axis_index("xh")
    column = lax.axis_index("xl")
    block = lax.axis_index("gz")
    for entry in range(32):
        table_ref[place_ref[line, entry // 4, block * 4 + entry % 4]] = jnp.int32(entry)

    def gather(slot, carry):
        entry = table_ref[column * 16 + slot]
        source = 2 * (entry // 4) + entry % 2
        rows = pl.ds(pl.multiple_of(slot * 16, 16), 16)
        for k in range(9):
            wide_ref[k, rows, :] = own_ref[source, k].astype(F32)
        return carry

    lax.fori_loop(0, 16, gather, 0, unroll=4)


def place_kernel(table_ref, other_ref, wide_ref, out_ref, work_ref, buf_ref, sems):
    column = lax.axis_index("xl")

    def gather(slot, carry):
        entry = table_ref[column * 16 + slot]
        source = 2 * (entry // 4) + entry % 2
        is_own = (entry % 4) // 2 == column
        rows = pl.ds(pl.multiple_of(slot * 16, 16), 16)
        for k in range(9):
            work_ref[k, rows, :] = jnp.where(is_own, wide_ref[k, rows, :], other_ref[source, k].astype(F32))
        return carry

    lax.fori_loop(0, 16, gather, 0, unroll=4)
    copies = []
    for k in range(9):
        for lane in range(16):
            buf_ref[k, :, lane * 128 : (lane + 1) * 128] = work_ref[k, pl.ds(lane, 16, stride=16), :]
        copies.append(pltpu.make_async_copy(buf_ref.at[k], out_ref.at[k], sems.at[k]))
        copies[k].start()
    for copy in copies:
        copy.wait()


def local(links, null_vectors, offsets, place):
    own = null_vectors[0, 0]
    links = links[0, 0]
    vmem = pl.BlockSpec(memory_space=pltpu.VMEM)
    smem = pl.BlockSpec(memory_space=pltpu.SMEM)
    anywhere = pl.BlockSpec(memory_space=pl.ANY)
    rows, packed = pl.pallas_call(
        prepare_kernel,
        out_shape=(
            jax.ShapeDtypeStruct((16, 64, 128), BF16),
            jax.ShapeDtypeStruct((4, 64, 256), BF16),
        ),
        in_specs=[vmem],
        out_specs=(vmem,) * 2,
        scratch_shapes=[pltpu.VMEM((512, 128), F32)],
        compiler_params=pltpu.CompilerParams(vmem_limit_bytes=16 * 1024 * 1024),
        cost_estimate=pl.CostEstimate(
            flops=2_000_000_000, bytes_accessed=10_000_000, transcendentals=0
        ),
        name="prepare",
    )(own)
    slabs = pl.pallas_call(
        slab_kernel,
        grid=(1,),
        out_shape=jax.ShapeDtypeStruct((4, 2, 32, 128), BF16),
        in_specs=[
            pl.BlockSpec((1, 2, 32, 128), lambda i: (0, 0, 0, 0)),
            pl.BlockSpec((1, 2, 32, 128), lambda i: (7, 0, 0, 0)),
        ],
        out_specs=pl.BlockSpec((4, 2, 32, 128), lambda i: (0, 0, 0, 0)),
        name="slabs",
    )(own, own)
    z_slabs = lax.all_to_all(slabs, "gz", 0, 0, tiled=True)
    y_low = lax.ppermute(own, GY, shift(16, 1))
    y_high = lax.ppermute(own, GY, shift(16, -1))
    x_low = lax.ppermute(own, GX, shift(16, 1))
    x_high = lax.ppermute(own, GX, shift(16, -1))
    part, acc, role_table = pl.pallas_call(
        inside_kernel,
        out_shape=(
            jax.ShapeDtypeStruct((4, 4, 16, 128), BF16),
            jax.ShapeDtypeStruct((4, 64, 64), F32),
            jax.ShapeDtypeStruct((9,), jnp.int32),
        ),
        in_specs=[smem] + [vmem] * 3,
        out_specs=(vmem, vmem, smem),
        scratch_shapes=[pltpu.VMEM((4, 1280, 64), BF16)],
        compiler_params=pltpu.CompilerParams(vmem_limit_bytes=16 * 1024 * 1024),
        cost_estimate=pl.CostEstimate(flops=150_000_000, bytes_accessed=3_000_000, transcendentals=0),
        name="inside",
    )(offsets.T, links, rows, packed)
    partial_value = pl.pallas_call(
        across_kernel,
        out_shape=jax.ShapeDtypeStruct((4, 9, 16, 128), BF16),
        in_specs=[smem] + [vmem] * 9,
        out_specs=vmem,
        scratch_shapes=[pltpu.VMEM((68, 64, 128), BF16), pltpu.VMEM((4, 1152, 64), BF16)],
        compiler_params=pltpu.CompilerParams(vmem_limit_bytes=16 * 1024 * 1024),
        cost_estimate=pl.CostEstimate(flops=150_000_000, bytes_accessed=3_000_000, transcendentals=0),
        name="across",
    )(role_table, links, x_low, x_high, y_low, y_high, z_slabs, part, acc, packed)
    parts = lax.all_to_all(partial_value, ("xl", "yp"), 0, 0, tiled=True)
    chunk = jnp.sum(parts.astype(F32), axis=0).astype(BF16)
    spread = jnp.broadcast_to(chunk[None], (16, 9, 16, 128))
    mine = lax.all_to_all(spread, GY, 0, 0, tiled=True)
    other = lax.ppermute(mine, "xl", swap_inner(2))
    wide, table = pl.pallas_call(
        gather_kernel,
        out_shape=(
            jax.ShapeDtypeStruct((9, 256, 128), F32),
            jax.ShapeDtypeStruct((32,), jnp.int32),
        ),
        in_specs=[smem, vmem],
        out_specs=(vmem, smem),
        compiler_params=pltpu.CompilerParams(vmem_limit_bytes=16 * 1024 * 1024),
        cost_estimate=pl.CostEstimate(flops=1_000_000, bytes_accessed=3_000_000, transcendentals=0),
        name="gather",
    )(place.reshape(8, 8, 16), mine)
    placed = pl.pallas_call(
        place_kernel,
        out_shape=jax.ShapeDtypeStruct((9, 16, 2048), F32),
        in_specs=[smem, vmem, vmem],
        out_specs=anywhere,
        scratch_shapes=[
            pltpu.VMEM((9, 256, 128), F32),
            pltpu.VMEM((9, 16, 2048), F32),
            pltpu.SemaphoreType.DMA((9,)),
        ],
        compiler_params=pltpu.CompilerParams(vmem_limit_bytes=32 * 1024 * 1024),
        name="place",
    )(table, other, wide)
    return jnp.transpose(placed, (1, 0, 2))[None, None]


def solution(mesh):
    fine = Mesh(mesh.devices.reshape(8, 2, 2, 4, 2, 4), ("xh", "xl", "yl", "yh", "yp", "gz"))
    placed = (P(GX, GY, "gz"), P(GX, GY, "gz"), P(), P())
    return jax.shard_map(
        local,
        mesh=fine,
        in_specs=placed,
        out_specs=P(GX, "gz"),
        check_vma=False,
    )
```

```python
import jax
import jax.numpy as jnp
from jax import lax
from jax.experimental import pallas as pl
from jax.experimental.pallas import tpu as pltpu
from jax.sharding import Mesh, PartitionSpec as P

F32 = jnp.float32
BF16 = jnp.bfloat16
GX = ("xh", "xl")
GY = ("yl", "yh", "yp")


def swap_inner(count):
    return [(i, i ^ 1) for i in range(count)]


def swap_outer(count):
    pairs = []
    for i in range(count):
        step = 1 if i % 2 else -1
        pairs.append((i, (i + step) % count))
    return pairs


def shift(count, step):
    return [(i, (i + step) % count) for i in range(count)]


def lane_index(shape):
    return lax.broadcasted_iota(jnp.int32, shape, 1)


def block_of(vectors, signs):
    return jnp.concatenate(
        [vectors * signs, jnp.concatenate([vectors[:, 64:], vectors[:, :64]], 1)], 0
    )


def lane_signs():
    return jnp.where(lane_index((32, 128)) < 64, 1.0, -1.0).astype(BF16)


def hop(link_block, rows):
    out = lax.dot_general(link_block, rows, (((1,), (1,)), ((), ())), preferred_element_type=F32)
    return out.astype(BF16)


def project(own, stacked):
    return jnp.dot(own, stacked, preferred_element_type=F32)


def fold(result):
    first = jnp.concatenate([result[0:16], result[16:32]], 1)
    second = jnp.concatenate([result[32:48], result[48:64]], 1)
    low = lane_index((16, 128)) % 64 < 32
    return first + jnp.where(low, pltpu.roll(second, 96, 1), -pltpu.roll(second, 32, 1))


def roles_of(role_ref):
    return role_ref[8], [role_ref[axis] for axis in range(4)], [role_ref[4 + axis] for axis in range(4)]


def slab_kernel(first_ref, last_ref, slab_ref):
    after = (lax.axis_index("gz") + 1) % 4
    for step in range(1, 4):
        slab_ref[(after + step) % 4] = first_ref[0]
    slab_ref[after] = last_ref[0]


def prepare_kernel(v_ref, rows_ref, own_ref, vf_ref):
    signs = lane_signs()
    for z in range(8):
        for t in range(2):
            vf_ref[pl.ds((2 * z + t) * 32, 32), :] = v_ref[z, t].astype(F32)
            rows_ref[2 * z + t] = block_of(v_ref[z, t], signs)
    low = lane_index((16, 128)) < 64
    for z in range(8):
        base = z * 64
        quarter = []
        for first in range(2):
            left = vf_ref[pl.ds(base + first, 16, stride=2), :]
            right = vf_ref[pl.ds(base + 32 + first, 16, stride=2), :]
            quarter.append(
                (
                    jnp.where(low, left, pltpu.roll(right, 64, 1)),
                    jnp.where(low, pltpu.roll(left, 64, 1), right),
                )
            )
        half = jnp.concatenate([quarter[0][0], quarter[1][0], quarter[0][1], quarter[1][1]], 0)
        lanes = slice((z % 2) * 128, (z % 2) * 128 + 128)
        own_ref[z // 2, :, lanes] = half.astype(BF16)


def inside_kernel(
    off_ref,
    links_ref,
    rows_ref,
    own_ref,
    part_ref,
    acc_ref,
    role_ref,
    hop_ref,
):
    k_self = jnp.int32(36)
    found = []
    for place, (axis, sign) in enumerate([(a, g) for g in (-1, 1) for a in range(4)]):
        index = jnp.int32(0)
        for k in range(9):
            index = index + jnp.where(off_ref[axis, k] == sign, k, 0).astype(jnp.int32)
        role_ref[place] = index
        found.append(index)
        k_self = k_self - index
    role_ref[8] = k_self
    minus, plus = found[:4], found[4:]
    for z in range(8):
        agg = z // 2
        for t in range(2):
            k_tin = plus[3] if t == 1 else minus[3]
            k_tout = minus[3] if t == 1 else plus[3]
            k_zin = minus[2] if z % 2 == 0 else plus[2]
            target = z - 1 if z % 2 == 0 else z + 1
            stack = [
                links_ref[z, t, k_self],
                links_ref[z, 1 - t, k_tin],
                links_ref[z ^ 1, t, k_zin],
                links_ref[z, 1 - t, k_tout],
            ]
            if 0 <= target <= 7:
                k_back = plus[2] if z % 2 == 0 else minus[2]
                stack.append(links_ref[target, t, k_back])
            res = hop(jnp.concatenate(stack, 0), rows_ref[2 * z + t])
            here = (2 * (z % 2) + t) * 64
            side = (2 * (z % 2) + 1 - t) * 64
            across = (2 * (1 - z % 2) + t) * 64
            hop_ref[agg, here : here + 64] = res[0:64]
            hop_ref[agg, 256 + side : 256 + side + 64] = res[64:128]
            hop_ref[agg, 512 + across : 512 + across + 64] = res[128:192]
            hop_ref[agg, 768 + side : 768 + side + 64] = res[192:256]
            if 0 <= target <= 7:
                row = 1024 + (2 * (target % 2) + t) * 64
                hop_ref[target // 2, row : row + 64] = res[256:320]
    first = jnp.where(lane_index((64, 256)) % 128 < 64, 1.0, 0.0).astype(BF16)
    second = jnp.where(lane_index((64, 256)) % 128 < 64, 0.0, 1.0).astype(BF16)
    for agg in range(4):
        own = own_ref[agg]
        acc_ref[agg] = project(jnp.concatenate([own] * 3, 1), hop_ref[agg, 0:768])
        part_ref[agg, 0] = fold(project(own * first, hop_ref[agg, 768:1024])).astype(BF16)
        part_ref[agg, 1] = fold(project(own * second, hop_ref[agg, 768:1024])).astype(BF16)
        if agg > 0:
            part_ref[agg, 2] = fold(project(own[:, :128], hop_ref[agg, 1024:1152])).astype(BF16)
        if agg < 3:
            part_ref[agg, 3] = fold(project(own[:, 128:], hop_ref[agg, 1152:1280])).astype(BF16)
    part_ref[0, 2] = jnp.zeros((16, 128), BF16)
    part_ref[3, 3] = jnp.zeros((16, 128), BF16)


def across_kernel(
    role_ref,
    links_ref,
    xl_ref,
    xh_ref,
    ya_ref,
    yb_ref,
    z_ref,
    part_ref,
    acc_ref,
    own_ref,
    out_ref,
    rows_ref,
    hop_ref,
):
    k_self, minus, plus = roles_of(role_ref)
    x_odd = lax.axis_index("xl")
    y_odd = lax.axis_index("yp")
    block = lax.axis_index("gz")
    x_out = jnp.where(x_odd == 1, plus[0], minus[0])
    x_in = jnp.where(x_odd == 1, minus[0], plus[0])
    y_out = jnp.where(y_odd == 1, plus[1], minus[1])
    y_in = jnp.where(y_odd == 1, minus[1], plus[1])
    x_base = pl.multiple_of(512 * x_odd, 256)
    zero = jnp.zeros((16, 128), BF16)
    signs = lane_signs()
    sides = (
        (xl_ref, minus[0], 512 - x_base),
        (xh_ref, plus[0], x_base),
        (ya_ref, y_in, 256),
        (yb_ref, y_out, 768),
    )
    for t in range(2):
        rows_ref[64 + t] = block_of(z_ref[(block + 3) % 4, t], signs)
        rows_ref[66 + t] = block_of(z_ref[(block + 1) % 4, t], signs)
    for z in range(8):
        for t in range(2):
            for role, (ref, _, _) in enumerate(sides):
                rows_ref[role * 16 + 2 * z + t] = block_of(ref[z, t], signs)
    for t in range(2):
        hop_ref[0, 1024 + t * 64 : 1088 + t * 64] = hop(links_ref[0, t, minus[2]], rows_ref[64 + t])
        hop_ref[3, 1024 + t * 64 : 1088 + t * 64] = hop(links_ref[7, t, plus[2]], rows_ref[66 + t])
    for z in range(8):
        for t in range(2):
            for role, (_, k, base) in enumerate(sides):
                row = base + (2 * (z % 2) + t) * 64
                row = row if isinstance(row, int) else pl.multiple_of(row, 64)
                res = hop(links_ref[z, t, k], rows_ref[role * 16 + 2 * z + t])
                hop_ref[z // 2, pl.ds(row, 64)] = res
    for agg in range(4):
        own = own_ref[agg]
        total = acc_ref[agg] + project(jnp.concatenate([own] * 2, 1), hop_ref[agg, 0:512])
        out_ref[agg, k_self] = fold(total).astype(BF16)
        out_ref[agg, x_out] = fold(project(own, hop_ref[agg, 512:768])).astype(BF16)
        out_ref[agg, y_out] = fold(project(own, hop_ref[agg, 768:1024])).astype(BF16)
        out_ref[agg, x_in] = zero
        out_ref[agg, y_in] = zero
        out_ref[agg, minus[3]] = part_ref[agg, 0]
        out_ref[agg, plus[3]] = part_ref[agg, 1]
        if agg > 0:
            out_ref[agg, minus[2]] = part_ref[agg, 2]
        else:
            out_ref[agg, minus[2]] = fold(project(own[:, :128], hop_ref[0, 1024:1152])).astype(BF16)
        if agg < 3:
            out_ref[agg, plus[2]] = part_ref[agg, 3]
        else:
            out_ref[agg, plus[2]] = fold(project(own[:, 128:], hop_ref[3, 1024:1152])).astype(BF16)


def gather_kernel(place_ref, own_ref, wide_ref, table_ref):
    line = lax.axis_index("xh")
    column = lax.axis_index("xl")
    block = lax.axis_index("gz")
    for entry in range(32):
        table_ref[place_ref[line, entry // 4, block * 4 + entry % 4]] = jnp.int32(entry)

    def gather(slot, carry):
        entry = table_ref[column * 16 + slot]
        source = 2 * (entry // 4) + entry % 2
        rows = pl.ds(pl.multiple_of(slot * 16, 16), 16)
        for k in range(9):
            wide_ref[k, rows, :] = own_ref[source, k].astype(F32)
        return carry

    lax.fori_loop(0, 16, gather, 0, unroll=4)


def place_kernel(table_ref, other_ref, wide_ref, out_ref, work_ref, buf_ref, sems):
    column = lax.axis_index("xl")

    def gather(slot, carry):
        entry = table_ref[column * 16 + slot]
        source = 2 * (entry // 4) + entry % 2
        is_own = (entry % 4) // 2 == column
        rows = pl.ds(pl.multiple_of(slot * 16, 16), 16)
        for k in range(9):
            work_ref[k, rows, :] = jnp.where(is_own, wide_ref[k, rows, :], other_ref[source, k].astype(F32))
        return carry

    lax.fori_loop(0, 16, gather, 0, unroll=4)
    copies = []
    for k in range(9):
        for lane in range(16):
            buf_ref[k, :, lane * 128 : (lane + 1) * 128] = work_ref[k, pl.ds(lane, 16, stride=16), :]
        copies.append(pltpu.make_async_copy(buf_ref.at[k], out_ref.at[k], sems.at[k]))
        copies[k].start()
    for copy in copies:
        copy.wait()


def local(links, null_vectors, offsets, place):
    own = null_vectors[0, 0]
    links = links[0, 0]
    vmem = pl.BlockSpec(memory_space=pltpu.VMEM)
    smem = pl.BlockSpec(memory_space=pltpu.SMEM)
    anywhere = pl.BlockSpec(memory_space=pl.ANY)
    rows, packed = pl.pallas_call(
        prepare_kernel,
        out_shape=(
            jax.ShapeDtypeStruct((16, 64, 128), BF16),
            jax.ShapeDtypeStruct((4, 64, 256), BF16),
        ),
        in_specs=[vmem],
        out_specs=(vmem,) * 2,
        scratch_shapes=[pltpu.VMEM((512, 128), F32)],
        compiler_params=pltpu.CompilerParams(vmem_limit_bytes=16 * 1024 * 1024),
        cost_estimate=pl.CostEstimate(flops=1_000_000, bytes_accessed=500_000, transcendentals=0),
        name="prepare",
    )(own)
    slabs = pl.pallas_call(
        slab_kernel,
        grid=(1,),
        out_shape=jax.ShapeDtypeStruct((4, 2, 32, 128), BF16),
        in_specs=[
            pl.BlockSpec((1, 2, 32, 128), lambda i: (0, 0, 0, 0)),
            pl.BlockSpec((1, 2, 32, 128), lambda i: (7, 0, 0, 0)),
        ],
        out_specs=pl.BlockSpec((4, 2, 32, 128), lambda i: (0, 0, 0, 0)),
        cost_estimate=pl.CostEstimate(
            flops=2_000_000_000, bytes_accessed=10_000_000, transcendentals=0
        ),
        name="slabs",
    )(own, own)
    z_slabs = lax.all_to_all(slabs, "gz", 0, 0, tiled=True)
    y_outer = lax.ppermute(own, GY, swap_outer(16))
    y_inner = lax.ppermute(own, "yp", swap_inner(2))
    x_low = lax.ppermute(own, GX, shift(16, 1))
    x_high = lax.ppermute(own, GX, shift(16, -1))
    part, acc, role_table = pl.pallas_call(
        inside_kernel,
        out_shape=(
            jax.ShapeDtypeStruct((4, 4, 16, 128), BF16),
            jax.ShapeDtypeStruct((4, 64, 64), F32),
            jax.ShapeDtypeStruct((9,), jnp.int32),
        ),
        in_specs=[smem] + [vmem] * 3,
        out_specs=(vmem, vmem, smem),
        scratch_shapes=[pltpu.VMEM((4, 1280, 64), BF16)],
        compiler_params=pltpu.CompilerParams(vmem_limit_bytes=16 * 1024 * 1024),
        cost_estimate=pl.CostEstimate(flops=150_000_000, bytes_accessed=3_000_000, transcendentals=0),
        name="inside",
    )(offsets.T, links, rows, packed)
    partial_value = pl.pallas_call(
        across_kernel,
        out_shape=jax.ShapeDtypeStruct((4, 9, 16, 128), BF16),
        in_specs=[smem] + [vmem] * 9,
        out_specs=vmem,
        scratch_shapes=[pltpu.VMEM((68, 64, 128), BF16), pltpu.VMEM((4, 1152, 64), BF16)],
        compiler_params=pltpu.CompilerParams(vmem_limit_bytes=16 * 1024 * 1024),
        cost_estimate=pl.CostEstimate(flops=150_000_000, bytes_accessed=3_000_000, transcendentals=0),
        name="across",
    )(role_table, links, x_low, x_high, y_inner, y_outer, z_slabs, part, acc, packed)
    parts = lax.all_to_all(partial_value, ("xl", "yp"), 0, 0, tiled=True)
    chunk = jnp.sum(parts.astype(F32), axis=0).astype(BF16)
    spread = jnp.broadcast_to(chunk[None], (16, 9, 16, 128))
    mine = lax.all_to_all(spread, GY, 0, 0, tiled=True)
    other = lax.ppermute(mine, "xl", swap_inner(2))
    wide, table = pl.pallas_call(
        gather_kernel,
        out_shape=(
            jax.ShapeDtypeStruct((9, 256, 128), F32),
            jax.ShapeDtypeStruct((32,), jnp.int32),
        ),
        in_specs=[smem, vmem],
        out_specs=(vmem, smem),
        compiler_params=pltpu.CompilerParams(vmem_limit_bytes=16 * 1024 * 1024),
        cost_estimate=pl.CostEstimate(flops=1_000_000, bytes_accessed=3_000_000, transcendentals=0),
        name="gather",
    )(place.reshape(8, 8, 16), mine)
    placed = pl.pallas_call(
        place_kernel,
        out_shape=jax.ShapeDtypeStruct((9, 16, 2048), F32),
        in_specs=[smem, vmem, vmem],
        out_specs=anywhere,
        scratch_shapes=[
            pltpu.VMEM((9, 256, 128), F32),
            pltpu.VMEM((9, 16, 2048), F32),
            pltpu.SemaphoreType.DMA((9,)),
        ],
        compiler_params=pltpu.CompilerParams(vmem_limit_bytes=32 * 1024 * 1024),
        name="place",
    )(table, other, wide)
    return jnp.transpose(placed, (1, 0, 2))[None, None]


def solution(mesh):
    fine = Mesh(mesh.devices.reshape(8, 2, 2, 4, 2, 4), ("xh", "xl", "yl", "yh", "yp", "gz"))
    placed = (P(GX, GY, "gz"), P(GX, GY, "gz"), P(), P())
    return jax.shard_map(
        local,
        mesh=fine,
        in_specs=placed,
        out_specs=P(GX, "gz"),
        check_vma=False,
    )
```
